256 devices in a mesh: leaf: 16 (over y_lo, x, core), samp: 16 (over z, y_hi).
Axes of the slice: x: 4, y: 4 (y_hi: 2, y_lo: 2; y = y_hi * 2 + y_lo), z: 8, core: 2. Of those that a mesh axis runs over, the one named last changes fastest.
Arguments:
- limits: float32 [8, 16, 512], P(None, 'leaf'), may hold values from -1.25 to 2.25
- inv_scale: float32 [8, 16, 512], P(None, 'leaf'), may hold values from 0.5 to 1.5
- lower_blocks: bfloat16 [8, 16, 512, 512], P(None, 'leaf'), may hold values from -0.19921875 to 0.19921875
- qmc_gen: int32 [8, 16, 512], P(None, 'leaf'), may hold values from 1 to 8191
- col_one: bfloat16 [8, 16, 512, 64], P(None, 'leaf'), may hold values from -0.75 to 0.75
- row_one: bfloat16 [8, 16, 512, 64], P(None, 'leaf'), may hold values from -0.25 to 0.25
- col_two: bfloat16 [8, 16, 512, 64], P(None, 'leaf'), may hold values from -0.75 to 0.75
- row_two: bfloat16 [8, 16, 512, 64], P(None, 'leaf'), may hold values from -0.25 to 0.25
Outputs:
- draws: bfloat16 [8, 16, 512, 8192], P(None, 'leaf', None, 'samp')
- mean_log: float32 [8, 16], P(None, 'leaf')
- sample_log: float32 [8192], P('samp')
The draws below stay inside these ranges and needn't reach their ends.
Inputs may be any that keep to these rules, and one draw needn't show every extreme that they name: `qmc_gen`: A rank-one lattice rule's generating vector.
All inputs are finite; a program needn't handle non-finite values.
Results may differ from the reference program's by a relative error of at most 0.006.
Values may be sent and summed in bfloat16 or wider, within the bound.
A program may use at most 64 MiB of HBM per device.

```python
import math
import jax
import jax.numpy as jnp
from jax import lax

M = 512
R = 64
SUB = 128
LEAF_DEV = 8
NODES = 16
SAMPLES = 8192


def draw_limits(key, part):
    key_level = jax.random.fold_in(key, 11)
    key_noise = jax.random.fold_in(key, 12)
    offset = jax.random.uniform(key_level, (LEAF_DEV, NODES, 1), jnp.float32)
    node = jnp.arange(NODES, dtype=jnp.float32)[None, :, None]
    position = (node + offset) / NODES
    level = -0.5 + 2.0 * position
    noise = jnp.clip(0.3 * jax.random.normal(key_noise, (LEAF_DEV, NODES, M), jnp.float32), -0.75, 0.75)
    return level + noise


def place_ends(result, key, smallest, top_value):
    place = [jax.random.randint(jax.random.fold_in(key, axis), (), 0, length) for axis, length in enumerate(result.shape)]
    widest = result.shape.index(max(result.shape))
    next_to = place[:widest] + [(place[widest] + 1) % result.shape[widest]] + place[widest + 1:]
    return result.at[tuple(place)].set(smallest).at[tuple(next_to)].set(top_value)


def levels(key, shape, shards, smallest, largest):
    loudness = 1.0
    for dim, shards_of in shards:
        steps = jax.random.uniform(jax.random.fold_in(jax.random.fold_in(key, 6), dim), (shards_of,), jnp.float32, smallest / len(shards), largest / len(shards))
        loudness = loudness * jnp.repeat(jnp.exp(steps), shape[dim] // shards_of).reshape((-1,) + (1,) * (len(shape) - 1 - dim))
    return loudness


def scatter_about(key, dims, deviation, bound, cuts=(), held_as=jnp.bfloat16):
    values = deviation * jax.random.normal(key, dims, jnp.float32)
    if cuts:
        values = values * levels(key, dims, cuts, -0.22, 0.18)
    return jnp.clip(values, -bound, bound).astype(held_as)


def setup_inputs(seed: int = 0) -> dict:
    arg_keys = jax.random.split(jax.random.key(seed), 9)
    limits = draw_limits(jax.random.fold_in(arg_keys[8], 71), 0)
    inv_scale = jnp.clip(jnp.exp(math.log(1.5) - 1.0986123 * jax.random.uniform(arg_keys[1], (LEAF_DEV, NODES, M), jnp.float32) ** levels(arg_keys[1], (LEAF_DEV, NODES, M), ((1, 16),), -0.2, 0.2)), 0.5, 1.5)
    lower_blocks = scatter_about(arg_keys[2], (LEAF_DEV, NODES, M, M), 0.04, 0.19921875, ((1, 16),))
    qmc_gen = place_ends(jax.random.randint(arg_keys[3], (LEAF_DEV, NODES, M), 1, SAMPLES), jax.random.fold_in(arg_keys[3], 1), 1, SAMPLES - 1).astype(jnp.int32)
    col_one = scatter_about(arg_keys[4], (LEAF_DEV, NODES, M, R), R ** -0.5, 0.75, ((1, 16),))
    row_one = scatter_about(arg_keys[5], (LEAF_DEV, NODES, M, R), M ** -0.5, 0.25, ((1, 16),))
    col_two = scatter_about(arg_keys[6], (LEAF_DEV, NODES, M, R), R ** -0.5, 0.75, ((1, 16),))
    row_two = scatter_about(arg_keys[7], (LEAF_DEV, NODES, M, R), M ** -0.5, 0.25, ((1, 16),))
    return dict(limits=limits, inv_scale=inv_scale, lower_blocks=lower_blocks, qmc_gen=qmc_gen, col_one=col_one, row_one=row_one, col_two=col_two, row_two=row_two)


coef_a = (-39.69683028665376, 220.9460984245205, -275.9285104469687, 138.357751867269, -30.66479806614716, 2.506628277459239)
coef_b = (-54.47609879822406, 161.5858368580409, -155.6989798598866, 66.80131188771972, -13.28068155288572)
coef_c = (-0.007784894002430293, -0.3223964580411365, -2.400758277161838, -2.549732539343734, 4.374664141464968, 2.938163982698783)
coef_d = (0.007784695709041462, 0.3224671290700398, 2.445134137142996, 3.754408661907416)
inv_root_two = 0.7071067811865476
split_low = 0.02425

def normal_cdf(value):
    return 0.5 * lax.erfc(-value * inv_root_two)

def log_normal_cdf(value):
    return jnp.log(normal_cdf(value))

def horner(coefs, value):
    total = coefs[0] + 0.0 * value
    for entry in coefs[1:]:
        total = total * value + entry
    return total

def tail_value(prob):
    safe = jnp.clip(prob, 1e-30, split_low)
    qvalue = jnp.sqrt(-2.0 * jnp.log(safe))
    return horner(coef_c, qvalue) / (horner(coef_d, qvalue) * qvalue + 1.0)

def normal_quantile(prob):
    centre = jnp.clip(prob, split_low, 1.0 - split_low) - 0.5
    square = centre * centre
    middle = horner(coef_a, square) * centre / (horner(coef_b, square) * square + 1.0)
    lower = tail_value(prob)
    upper = -tail_value(1.0 - prob)
    return jnp.where(prob < split_low, lower, jnp.where(prob > 1.0 - split_low, upper, middle))

def leaf_pass(lower_leaf, scale_leaf, limit_leaf, points, shift_all):
    pieces = []
    logsum = jnp.zeros((points.shape[1],), jnp.float32)
    for block in range(M // SUB):
        row_begin = block * SUB
        row_end = row_begin + SUB
        centred = limit_leaf[row_begin:row_end, None] - shift_all[row_begin:row_end]
        if block > 0:
            earlier = jnp.concatenate(pieces, axis=0)
            centred = centred - jnp.dot(lower_leaf[row_begin:row_end, :row_begin], earlier, preferred_element_type=jnp.float32)
        scaled = jnp.maximum(scale_leaf[row_begin:row_end, None] * centred, -6.0)
        sample_block = normal_quantile(points[row_begin:row_end] * normal_cdf(scaled)).astype(jnp.bfloat16)
        logsum = logsum + lax.optimization_barrier(jnp.sum(log_normal_cdf(scaled), axis=0))
        pieces.append(sample_block)
    return (jnp.concatenate(pieces, axis=0), logsum)

def points_of(generator):
    sample_index = jnp.arange(SAMPLES, dtype=jnp.int32)
    residue = sample_index[None, :] * generator[:, None].astype(jnp.int32) % SAMPLES
    return (residue.astype(jnp.float32) + 0.5) / SAMPLES

def shift_of(col_leaf, coef_leaf):
    return jnp.dot(col_leaf, coef_leaf, preferred_element_type=jnp.float32)

def reference(limits, inv_scale, lower_blocks, qmc_gen, col_one, row_one, col_two, row_two):
    count = LEAF_DEV * NODES

    def flatten(array):
        return array.reshape((count,) + array.shape[2:])
    lower_flat = flatten(lower_blocks)
    scale_flat = flatten(inv_scale)
    limit_flat = flatten(limits)
    gen_flat = flatten(qmc_gen)
    zero_shift = jnp.zeros((M, SAMPLES), jnp.float32)

    def first_pass(leaf_args):
        lower_leaf, scale_leaf, limit_leaf, gen_leaf, row_leaf = leaf_args
        draws_a, unused = leaf_pass(lower_leaf, scale_leaf, limit_leaf, points_of(gen_leaf), zero_shift)
        return jnp.dot(row_leaf.T, draws_a, preferred_element_type=jnp.float32).astype(jnp.bfloat16)
    coef_all = lax.map(first_pass, (lower_flat, scale_flat, limit_flat, gen_flat, flatten(row_one)))
    coef_sibling = jnp.flip(coef_all.reshape(LEAF_DEV, NODES // 2, 2, R, SAMPLES), axis=2).reshape(count, R, SAMPLES)

    def second_pass(leaf_args):
        lower_leaf, scale_leaf, limit_leaf, gen_leaf, col_leaf, coef_leaf, row_leaf = leaf_args
        draws_b, unused = leaf_pass(lower_leaf, scale_leaf, limit_leaf, points_of(gen_leaf), shift_of(col_leaf, coef_leaf))
        return jnp.dot(row_leaf.T, draws_b, preferred_element_type=jnp.float32)
    partial_all = lax.map(second_pass, (lower_flat, scale_flat, limit_flat, gen_flat, flatten(col_one), coef_sibling, flatten(row_two)))
    grouped = partial_all.reshape(LEAF_DEV, NODES // 4, 2, 2, R, SAMPLES)
    pair_sum = (grouped[:, :, :, 0] + grouped[:, :, :, 1]).astype(jnp.bfloat16)
    group_sum = jnp.flip(pair_sum, axis=2)
    group_sum = jnp.broadcast_to(group_sum[:, :, :, None], grouped.shape).reshape(count, R, SAMPLES)

    def third_pass(leaf_args):
        lower_leaf, scale_leaf, limit_leaf, gen_leaf, col_a, coef_first, col_b, coef_second = leaf_args
        shift_all = shift_of(col_a, coef_first) + shift_of(col_b, coef_second)
        return leaf_pass(lower_leaf, scale_leaf, limit_leaf, points_of(gen_leaf), shift_all)
    draws_c, logsum = lax.map(third_pass, (lower_flat, scale_flat, limit_flat, gen_flat, flatten(col_one), coef_sibling, flatten(col_two), group_sum))
    draws = draws_c.reshape(LEAF_DEV, NODES, M, SAMPLES)
    peak = lax.optimization_barrier(jnp.max(logsum, axis=1))
    mass = lax.optimization_barrier(jnp.sum(jnp.exp(logsum - peak[:, None]), axis=1))
    mean_log = ((peak + jnp.log(mass / SAMPLES)) / M).reshape(LEAF_DEV, NODES)
    sample_log = lax.optimization_barrier(jnp.sum(logsum, axis=0)) / (LEAF_DEV * NODES * M)
    return (draws, mean_log, sample_log)
```

```python
import functools
import math

import jax
import jax.numpy as jnp
from jax import lax
from jax.experimental import pallas as pl
from jax.experimental.pallas import tpu as pltpu
from jax.sharding import PartitionSpec as P

LEAVES = 8
M = 512
R = 64
SUB = 128
COLS = 512
HALF = 256
CHUNK = 16
TOTAL = 8192
MESH = pl.DeviceIdType.MESH

coef_a = (
    -39.69683028665376,
    220.9460984245205,
    -275.9285104469687,
    138.357751867269,
    -30.66479806614716,
    2.506628277459239,
)
coef_b = (
    -54.47609879822406,
    161.5858368580409,
    -155.6989798598866,
    66.80131188771972,
    -13.28068155288572,
    1.0,
)
coef_c = (
    -0.007784894002430293,
    -0.3223964580411365,
    -2.400758277161838,
    -2.549732539343734,
    4.374664141464968,
    2.938163982698783,
)
coef_d = (0.007784695709041462, 0.3224671290700398, 2.445134137142996, 3.754408661907416, 1.0)
split_low = 0.02425

K = coef_a[0] / coef_b[0]
G = math.sqrt(2.0 * math.log(2.0))
TAIL = -coef_c[0] * G / coef_d[0]
mono_a = tuple(v / coef_a[0] * K ** (2 * j) for j, v in enumerate(coef_a))
mono_b = tuple(v / coef_b[0] * K ** (2 * j) for j, v in enumerate(coef_b))
mono_c = tuple(v / coef_c[0] * G**-j for j, v in enumerate(coef_c))
mono_d = tuple(v / coef_d[0] * G**-j for j, v in enumerate(coef_d))

ROOT_HALF = math.sqrt(0.5)
FLOOR = -6.0 * ROOT_HALF
ERFC_FROM = -3.0 * ROOT_HALF
erfc_log2 = (
    0.0003123880466,
    0.00671664281,
    0.06322885333,
    -1.09054892,
    1.442791442,
    -0.08385716881,
)


def twice_cdf(z):
    tail = jnp.full_like(z, erfc_log2[0])
    tail = z * erfc_log2[0] + erfc_log2[1]
    for entry in erfc_log2[2:]:
        tail = tail * z + entry
    return jnp.where(z < ERFC_FROM, lax.exp2(tail), lax.erf(z) + 1.0)


def quantile(p):
    centre = p - 0.5 * K
    square = centre * centre
    small = jnp.minimum(p, K - p)
    tail = small < K * split_low
    depth = math.log2(K) - jnp.log2(small)
    depth = depth * lax.rsqrt(depth)
    var = jnp.where(tail, depth, square)
    top = var + jnp.where(tail, mono_c[1], mono_a[1])
    for c, a in zip(mono_c[2:], mono_a[2:]):
        top = top * var + jnp.where(tail, c, a)
    low = jnp.where(tail, 1.0, square + mono_b[1])
    for d, b in zip(mono_d[1:], mono_b[2:]):
        low = low * var + jnp.where(tail, d, b)
    scale = jnp.where(tail, jnp.where(centre < 0.0, -TAIL, TAIL), centre)
    return scale * top / low


def kernel(
    limits,
    scales,
    lower_hbm,
    gens,
    col_one_hbm,
    row_one_hbm,
    col_two_hbm,
    row_two_hbm,
    draws_hbm,
    mean_out,
    sample_out,
    lower,
    col_one,
    row_one,
    col_two,
    row_two,
    points,
    limit_b,
    scale_b,
    acc_0,
    acc_1,
    draw_0,
    draw_1,
    log_0,
    log_1,
    first_send,
    first_recv,
    second_send,
    second_recv,
    pair_send,
    pair_recv,
    stat_all,
    sums_all,
    load_sem,
    out_sem,
    first_sems,
    second_sems,
    pair_sems,
    stat_sems,
    sums_sems,
):
    leaf = lax.axis_index("leaf")
    samp = lax.axis_index("samp")
    n_leaf = lax.axis_size("leaf")
    n_samp = lax.axis_size("samp")
    sibling = leaf + 1 - 2 * lax.rem(leaf, 2)
    across = leaf + 2 - 4 * lax.rem(leaf // 2, 2)
    acc = (acc_0, acc_1)
    draw = (draw_0, draw_1)
    log_sum = (log_0, log_1)

    loads = (
        (lower_hbm, lower),
        (col_one_hbm, col_one),
        (row_one_hbm, row_one),
        (col_two_hbm, col_two),
        (row_two_hbm, row_two),
    )

    def load(which, i):
        src, dst = loads[which]
        return pltpu.make_async_copy(src.at[i, 0], dst.at[i], load_sem.at[which, i])

    def start_loads(which):
        def body(i, carry):
            load(which, i).start()
            return carry

        lax.fori_loop(0, LEAVES, body, 0)

    start_loads(0)
    start_loads(2)
    start_loads(1)
    start_loads(4)
    start_loads(3)

    barrier = pltpu.get_barrier_semaphore()

    def greet_leaf(d, carry):
        pl.semaphore_signal(
            barrier, inc=1, device_id={"leaf": lax.rem(leaf + d, n_leaf)}, device_id_type=MESH
        )
        return carry

    def greet_samp(d, carry):
        pl.semaphore_signal(
            barrier, inc=1, device_id={"samp": lax.rem(samp + d, n_samp)}, device_id_type=MESH
        )
        return carry

    lax.fori_loop(1, n_leaf, greet_leaf, 0)
    lax.fori_loop(1, n_samp, greet_samp, 0)

    def first_copy(i):
        return pltpu.make_async_remote_copy(
            src_ref=first_send.at[i],
            dst_ref=first_recv.at[i],
            send_sem=first_sems.at[0, i],
            recv_sem=first_sems.at[1, i],
            device_id={"leaf": sibling},
            device_id_type=MESH,
        )

    def second_copy(i):
        return pltpu.make_async_remote_copy(
            src_ref=second_send.at[i],
            dst_ref=second_recv.at[i],
            send_sem=second_sems.at[0, i],
            recv_sem=second_sems.at[1, i],
            device_id={"leaf": sibling},
            device_id_type=MESH,
        )

    def pair_copy(i):
        return pltpu.make_async_remote_copy(
            src_ref=pair_send.at[i],
            dst_ref=pair_recv.at[i],
            send_sem=pair_sems.at[0, i],
            recv_sem=pair_sems.at[1, i],
            device_id={"leaf": across},
            device_id_type=MESH,
        )

    def out_copy(i, h):
        return pltpu.make_async_copy(
            draw[h].at[lax.rem(i, 2)],
            draws_hbm.at[i, 0, :, pl.ds(h * HALF, HALF)],
            out_sem.at[h, i],
        )

    def spread(row):
        return jnp.broadcast_to(row, (SUB, SUB)).T

    def product(step, i, s, h):
        rows = slice(s * SUB, (s + 1) * SUB)
        cols = slice(h * HALF, (h + 1) * HALF)
        left, right = [], []
        if step > 0:
            left.append(
                jnp.concatenate([col_one[i, rows, :], col_two[i, rows, :]], axis=1)
            )
            right.append(first_recv[i, :, cols])
            if step == 1:
                right.append(jnp.zeros((R, HALF), jnp.bfloat16))
            else:
                right.append(pair_recv[i, :, cols])
        if s > 0:
            left.append(lower[i, rows, : s * SUB])
            right.append(draw[h][lax.rem(i, 2), : s * SUB, :])
        if not left:
            return
        a = left[0] if len(left) == 1 else jnp.concatenate(left, axis=1)
        b = right[0] if len(right) == 1 else jnp.concatenate(right, axis=0)
        acc[h][...] = jnp.dot(a, b, preferred_element_type=jnp.float32)

    def elementwise(step, i, s, h, gen_b):
        par = lax.rem(i, 2)
        total = None
        group = []
        for chunk in range(SUB // CHUNK):
            at = s * SUB + chunk * CHUNK
            rows = slice(at, at + CHUNK)
            cols = slice(h * HALF, (h + 1) * HALF)
            here = slice(chunk * CHUNK, (chunk + 1) * CHUNK)
            limit = limit_b[i, rows, :]
            scale = scale_b[i, rows, :]
            if step == 0 and s == 0:
                y = twice_cdf(jnp.maximum(scale * limit, FLOOR))
                y = jnp.concatenate([y, y], axis=1)
            else:
                limit = jnp.concatenate([limit, limit], axis=1)
                scale = jnp.concatenate([scale, scale], axis=1)
                z = jnp.maximum(scale * (limit - acc[h][here, :]), FLOOR)
                y = twice_cdf(z)
            if step == 0:
                g = gen_b[here, :]
                g = jnp.concatenate([g, g], axis=1)
                n = (
                    lax.broadcasted_iota(jnp.int32, (CHUNK, HALF), 1)
                    + (samp * COLS + h * HALF)
                )
                residue = jnp.bitwise_and(g * n, TOTAL - 1).astype(jnp.float32)
                u = residue * (0.5 * K / TOTAL) + 0.25 * K / TOTAL
                points[i, rows, cols] = u
            else:
                u = points[i, rows, cols]
            draw[h][par, rows, :] = quantile(u * y).astype(jnp.bfloat16)
            if step == 2:
                group.append(y[:8] * y[8:])
                if len(group) == 2:
                    term = jnp.log2(group[0] * group[1])
                    total = term if total is None else total + term
                    group = []
        if step == 2:
            if s == 0:
                log_sum[h][i] = total
            else:
                log_sum[h][i] += total

    units = [(s, h) for s in range(M // SUB) for h in range(2)]

    def leaf_pass(step, i, hooks):
        for at, (s, h) in enumerate(units):
            if at in hooks:
                hooks[at]()
            if at + 1 < len(units):
                product(step, i, *units[at + 1])
            gen_b = None
            if step == 0:
                row = gens[i, :, s * SUB : (s + 1) * SUB].astype(jnp.float32)
                gen_b = spread(row).astype(jnp.int32)
            elementwise(step, i, s, h, gen_b)

    def contract(basis, i):
        par = lax.rem(i, 2)
        both = jnp.concatenate([draw_0[par], draw_1[par]], axis=1)
        return lax.dot_general(
            basis[i], both, (((0,), (0,)), ((), ())), preferred_element_type=jnp.float32
        )

    def pass_a(i, carry):
        for s in range(M // SUB):
            cols = slice(s * SUB, (s + 1) * SUB)
            limit_b[i, cols, :] = spread(limits[i, :, cols])
            scale_b[i, cols, :] = spread(scales[i, :, cols] * ROOT_HALF)
        load(0, i).wait()
        load(2, i).wait()

        def send():
            @pl.when(i == 1)
            def _():
                pl.semaphore_wait(barrier, n_leaf + n_samp - 2)

            @pl.when(i >= 1)
            def _():
                first_copy(i - 1).start()

        leaf_pass(0, i, {2: send})
        first_send[i] = contract(row_one, i).astype(jnp.bfloat16)
        return carry

    lax.fori_loop(0, LEAVES, pass_a, 0)

    def pass_b(i, carry):
        load(1, i).wait()
        load(3, i).wait()
        load(4, i).wait()
        first_copy(i).wait_recv()

        def send():
            @pl.when(i == 0)
            def _():
                first_copy(LEAVES - 1).start()

            @pl.when(i >= 1)
            def _():
                second_copy(i - 1).start()

        def pair():
            @pl.when(i >= 2)
            def _():
                add_pair(i - 2)

        def send_pair():
            @pl.when(i >= 2)
            def _():
                pair_copy(i - 2).start()

        product(1, i, *units[0])
        leaf_pass(1, i, {1: pair, 2: send, 3: send_pair})
        second_send[i] = contract(row_two, i)
        return carry

    def add_pair(i):
        second_copy(i).wait_recv()
        pair_send[i] = (second_send[i] + second_recv[i]).astype(jnp.bfloat16)

    lax.fori_loop(0, LEAVES, pass_b, 0)

    def pass_c(i, carry):
        pair_copy(i).wait_recv()

        @pl.when(i >= 2)
        def _():
            out_copy(i - 2, 0).wait()
            out_copy(i - 2, 1).wait()

        def send():
            @pl.when(i == 0)
            def _():
                second_copy(LEAVES - 1).start()

        def pair():
            @pl.when(i < 2)
            def _():
                add_pair(i + LEAVES - 2)

        def send_pair():
            @pl.when(i < 2)
            def _():
                pair_copy(i + LEAVES - 2).start()

        product(2, i, *units[0])
        leaf_pass(2, i, {1: pair, 2: send, 3: send_pair})
        out_copy(i, 0).start()
        out_copy(i, 1).start()
        return carry

    lax.fori_loop(0, LEAVES, pass_c, 0)

    logsum = jnp.concatenate(
        [jnp.sum(log_0[...], axis=1), jnp.sum(log_1[...], axis=1)], axis=1
    )
    logsum = (logsum - float(M)) * math.log(2.0)
    peak = jnp.max(logsum, axis=1, keepdims=True)
    mass = jnp.sum(jnp.exp(logsum - peak), axis=1, keepdims=True)
    lane = lax.broadcasted_iota(jnp.int32, (LEAVES, SUB), 1)
    stat_all[samp] = jnp.where(lane == 0, peak, mass)
    sums_all[leaf] = jnp.sum(logsum, axis=0, keepdims=True)

    def stat_copy(d):
        to = lax.rem(samp + d, n_samp)
        return pltpu.make_async_remote_copy(
            src_ref=stat_all.at[samp],
            dst_ref=stat_all.at[samp],
            send_sem=stat_sems.at[0, d],
            recv_sem=stat_sems.at[1, d],
            device_id={"samp": to},
            device_id_type=MESH,
        )

    def sums_copy(d):
        to = lax.rem(leaf + d, n_leaf)
        return pltpu.make_async_remote_copy(
            src_ref=sums_all.at[leaf],
            dst_ref=sums_all.at[leaf],
            send_sem=sums_sems.at[0, d],
            recv_sem=sums_sems.at[1, d],
            device_id={"leaf": to},
            device_id_type=MESH,
        )

    def each(copy, what, count):
        def body(d, carry):
            what(copy(d))
            return carry

        lax.fori_loop(1, count, body, 0)

    each(stat_copy, lambda c: c.start(), n_samp)
    each(sums_copy, lambda c: c.start(), n_leaf)

    def drain(i, carry):
        first_copy(i).wait_send()
        second_copy(i).wait_send()
        pair_copy(i).wait_send()
        return carry

    lax.fori_loop(0, LEAVES, drain, 0)
    for i in (LEAVES - 2, LEAVES - 1):
        out_copy(i, 0).wait()
        out_copy(i, 1).wait()
    each(stat_copy, lambda c: c.wait(), n_samp)
    each(sums_copy, lambda c: c.wait(), n_leaf)

    stats = stat_all[...]
    peaks = stats[:, :, 0:1]
    top = jnp.max(peaks, axis=0)
    whole = jnp.sum(stats[:, :, 1:2] * jnp.exp(peaks - top[None]), axis=0)
    mean_out[...] = (top + jnp.log(whole / TOTAL)) / M
    sample_out[...] = jnp.sum(sums_all[...], axis=0) / (LEAVES * n_leaf * M)


def per_device(limits, inv_scale, lower_blocks, qmc_gen, col_one, row_one, col_two, row_two):
    vmem = pl.BlockSpec(memory_space=pltpu.VMEM)
    anywhere = pl.BlockSpec(memory_space=pl.ANY)
    f32, bf16 = jnp.float32, jnp.bfloat16
    n_leaf, n_samp = lax.axis_size("leaf"), lax.axis_size("samp")
    dma = pltpu.SemaphoreType.DMA
    draws, mean_log, sample_log = pl.pallas_call(
        kernel,
        out_shape=(
            jax.ShapeDtypeStruct((LEAVES, 1, M, COLS), bf16),
            jax.ShapeDtypeStruct((LEAVES, 1), f32),
            jax.ShapeDtypeStruct((1, COLS), f32),
        ),
        in_specs=[vmem, vmem, anywhere, vmem, anywhere, anywhere, anywhere, anywhere],
        out_specs=(anywhere, vmem, vmem),
        scratch_shapes=[
            pltpu.VMEM((LEAVES, M, M), bf16),
            pltpu.VMEM((LEAVES, M, R), bf16),
            pltpu.VMEM((LEAVES, M, R), bf16),
            pltpu.VMEM((LEAVES, M, R), bf16),
            pltpu.VMEM((LEAVES, M, R), bf16),
            pltpu.VMEM((LEAVES, M, COLS), f32),
            pltpu.VMEM((LEAVES, M, SUB), f32),
            pltpu.VMEM((LEAVES, M, SUB), f32),
            pltpu.VMEM((SUB, HALF), f32),
            pltpu.VMEM((SUB, HALF), f32),
            pltpu.VMEM((2, M, HALF), bf16),
            pltpu.VMEM((2, M, HALF), bf16),
            pltpu.VMEM((LEAVES, 8, HALF), f32),
            pltpu.VMEM((LEAVES, 8, HALF), f32),
            pltpu.VMEM((LEAVES, R, COLS), bf16),
            pltpu.VMEM((LEAVES, R, COLS), bf16),
            pltpu.VMEM((LEAVES, R, COLS), f32),
            pltpu.VMEM((LEAVES, R, COLS), f32),
            pltpu.VMEM((LEAVES, R, COLS), bf16),
            pltpu.VMEM((LEAVES, R, COLS), bf16),
            pltpu.VMEM((n_samp, LEAVES, SUB), f32),
            pltpu.VMEM((n_leaf, 1, COLS), f32),
            dma((5, LEAVES)),
            dma((2, LEAVES)),
            dma((2, LEAVES)),
            dma((2, LEAVES)),
            dma((2, LEAVES)),
            dma((2, n_samp)),
            dma((2, n_leaf)),
        ],
        compiler_params=pltpu.CompilerParams(
            collective_id=0, has_side_effects=True, vmem_limit_bytes=60 * 1024 * 1024
        ),
        name="conditioning",
    )(limits, inv_scale, lower_blocks, qmc_gen, col_one, row_one, col_two, row_two)
    return draws, mean_log, sample_log[0]


def solution(mesh):
    return jax.shard_map(
        per_device,
        mesh=mesh,
        in_specs=(
            P(None, "leaf", None),
            P(None, "leaf", None),
            P(None, "leaf", None, None),
            P(None, "leaf", None),
            P(None, "leaf", None, None),
            P(None, "leaf", None, None),
            P(None, "leaf", None, None),
            P(None, "leaf", None, None),
        ),
        out_specs=(P(None, "leaf", None, "samp"), P(None, "leaf"), P("samp")),
        check_vma=False,
    )
```

```python
import functools
import math

import jax
import jax.numpy as jnp
from jax import lax
from jax.experimental import pallas as pl
from jax.experimental.pallas import tpu as pltpu
from jax.sharding import PartitionSpec as P

LEAVES = 8
M = 512
R = 64
SUB = 128
COLS = 512
HALF = 256
CHUNK = 16
TOTAL = 8192
MESH = pl.DeviceIdType.MESH

coef_a = (
    -39.69683028665376,
    220.9460984245205,
    -275.9285104469687,
    138.357751867269,
    -30.66479806614716,
    2.506628277459239,
)
coef_b = (
    -54.47609879822406,
    161.5858368580409,
    -155.6989798598866,
    66.80131188771972,
    -13.28068155288572,
    1.0,
)
coef_c = (
    -0.007784894002430293,
    -0.3223964580411365,
    -2.400758277161838,
    -2.549732539343734,
    4.374664141464968,
    2.938163982698783,
)
coef_d = (0.007784695709041462, 0.3224671290700398, 2.445134137142996, 3.754408661907416, 1.0)
split_low = 0.02425

K = coef_a[0] / coef_b[0]
G = math.sqrt(2.0 * math.log(2.0))
EDGE = K * (0.5 - split_low)
TAIL = -coef_c[0] * G / coef_d[0]
mono_a = tuple(v / coef_a[0] * K ** (2 * j) for j, v in enumerate(coef_a))
mono_b = tuple(v / coef_b[0] * K ** (2 * j) for j, v in enumerate(coef_b))
mono_c = tuple(v / coef_c[0] * G**-j for j, v in enumerate(coef_c))
mono_d = tuple(EDGE / TAIL * v / coef_d[0] * G**-j for j, v in enumerate(coef_d))

ROOT_HALF = math.sqrt(0.5)
FLOOR = -6.0 * ROOT_HALF
ERFC_FROM = -3.5 * ROOT_HALF
erfc_log2 = (
    0.001479457231,
    0.02841664334,
    -1.205206352,
    1.255708033,
    -0.2048280003,
)


def twice_cdf(z):
    tail = z * erfc_log2[0] + erfc_log2[1]
    for entry in erfc_log2[2:]:
        tail = tail * z + entry
    return jnp.where(z < ERFC_FROM, lax.exp2(tail), lax.erf(z) + 1.0)


def quantile(p, centre_coefs):
    mono = [tile(c, p.shape) for c in centre_coefs]
    centre = p - 0.5 * K
    square = centre * centre
    small = jnp.minimum(p, K - p)
    tail = small < K * split_low
    depth = math.log2(K) - jnp.log2(small)
    depth = depth * lax.rsqrt(depth)
    var = jnp.where(tail, depth, square)
    top = var + jnp.where(tail, mono_c[1], mono[0])
    for c, a in zip(mono_c[2:], mono[1:5]):
        top = top * var + jnp.where(tail, c, a)
    low = jnp.where(tail, mono_d[0], square + mono_b[1])
    for d, b in zip(mono_d[1:], mono[5:]):
        low = low * var + jnp.where(tail, d, b)
    scale = jnp.clip(centre, -EDGE, EDGE)
    return scale * top / low


def tile(block, shape):
    block = jnp.concatenate([block] * (shape[1] // 128), axis=1)
    return jnp.concatenate([block] * (shape[0] // 8), axis=0)


def kernel(
    limits,
    scales,
    lower_hbm,
    gens,
    col_one_hbm,
    row_one_hbm,
    col_two_hbm,
    row_two_hbm,
    draws_hbm,
    mean_out,
    sample_out,
    lower,
    cols_t,
    row_one,
    row_two,
    cols_b,
    cols_c,
    tops,
    table,
    points,
    scale_b,
    acc_0,
    acc_1,
    draw_0,
    draw_1,
    log_0,
    log_1,
    first_send,
    first_recv,
    second_send,
    second_recv,
    pair_send,
    pair_recv,
    stat_all,
    sums_all,
    load_sem,
    out_sem,
    first_sems,
    second_sems,
    pair_sems,
    stat_sems,
    sums_sems,
):
    leaf = lax.axis_index("leaf")
    samp = lax.axis_index("samp")
    n_leaf = lax.axis_size("leaf")
    n_samp = lax.axis_size("samp")
    sibling = leaf + 1 - 2 * lax.rem(leaf, 2)
    across = leaf + 2 - 4 * lax.rem(leaf // 2, 2)
    acc = (acc_0, acc_1)
    draw = (draw_0, draw_1)
    log_sum = (log_0, log_1)

    loads = (
        (lower_hbm, lower),
        (row_one_hbm, row_one),
        (row_two_hbm, row_two),
        (col_one_hbm, cols_t),
        (col_two_hbm, cols_t),
    )

    def load(which, i):
        src, dst = loads[which]
        dst = dst.at[i]
        if which == 3:
            dst = dst.at[:R]
        if which == 4:
            dst = dst.at[R:]
        return pltpu.make_async_copy(src.at[i, 0], dst, load_sem.at[which, i])

    def start_loads(which):
        def body(i, carry):
            load(which, i).start()
            return carry

        lax.fori_loop(0, LEAVES, body, 0)

    for which in (0, 3, 4, 1, 2):
        start_loads(which)
    for at, value in enumerate(mono_a[1:] + mono_b[2:]):
        table[at] = jnp.full((8, 128), value, jnp.float32)
    for h in range(2):
        draw[h][1] = jnp.zeros((M, HALF), jnp.bfloat16)
    row = lax.broadcasted_iota(jnp.int32, (SUB, HALF), 0)
    ones_row = jnp.where(row < 3, 1.0, 0.0).astype(jnp.bfloat16)

    barrier = pltpu.get_barrier_semaphore()

    def greet_leaf(d, carry):
        pl.semaphore_signal(
            barrier, inc=1, device_id={"leaf": lax.rem(leaf + d, n_leaf)}, device_id_type=MESH
        )
        return carry

    def greet_samp(d, carry):
        pl.semaphore_signal(
            barrier, inc=1, device_id={"samp": lax.rem(samp + d, n_samp)}, device_id_type=MESH
        )
        return carry

    lax.fori_loop(1, n_leaf, greet_leaf, 0)
    lax.fori_loop(1, n_samp, greet_samp, 0)

    def first_copy(i):
        return pltpu.make_async_remote_copy(
            src_ref=first_send.at[i],
            dst_ref=first_recv.at[i],
            send_sem=first_sems.at[0, i],
            recv_sem=first_sems.at[1, i],
            device_id={"leaf": sibling},
            device_id_type=MESH,
        )

    def second_copy(i):
        return pltpu.make_async_remote_copy(
            src_ref=second_send.at[i],
            dst_ref=second_recv.at[i],
            send_sem=second_sems.at[0, i],
            recv_sem=second_sems.at[1, i],
            device_id={"leaf": sibling},
            device_id_type=MESH,
        )

    def pair_copy(i):
        return pltpu.make_async_remote_copy(
            src_ref=pair_send.at[i],
            dst_ref=pair_recv.at[i],
            send_sem=pair_sems.at[0, i],
            recv_sem=pair_sems.at[1, i],
            device_id={"leaf": across},
            device_id_type=MESH,
        )

    def out_copy(i, h):
        return pltpu.make_async_copy(
            draw[h].at[lax.rem(i, 2)],
            draws_hbm.at[i, 0, :, pl.ds(h * HALF, HALF)],
            out_sem.at[h, i],
        )

    def spread(row):
        return jnp.broadcast_to(row, (SUB, SUB)).T

    def product(step, i, s, h):
        rows = slice(s * SUB, (s + 1) * SUB)
        cols = slice(h * HALF, (h + 1) * HALF)
        left, right = [], []
        if step == 1:
            left.append(cols_b[i, rows, :])
            right += [first_recv[i, :, cols], ones_row[:R]]
        if step == 2:
            left.append(cols_c[i, rows, :])
            right += [first_recv[i, :, cols], pair_recv[i, :, cols]]
        if step != 1:
            left.append(tops[i, rows, :])
            right.append(ones_row)
        if s > 0:
            left.append(lower[i, rows, : s * SUB])
            right.append(draw[h][lax.rem(i, 2), : s * SUB, :])
        a = left[0] if len(left) == 1 else jnp.concatenate(left, axis=1)
        b = right[0] if len(right) == 1 else jnp.concatenate(right, axis=0)
        acc[h][...] = jnp.dot(a, b, preferred_element_type=jnp.float32)

    def elementwise(step, i, s, h, gen_b, limit_0):
        par = lax.rem(i, 2)
        total = None
        group = []
        for chunk in range(SUB // CHUNK):
            at = s * SUB + chunk * CHUNK
            rows = slice(at, at + CHUNK)
            cols = slice(h * HALF, (h + 1) * HALF)
            here = slice(chunk * CHUNK, (chunk + 1) * CHUNK)
            scale = scale_b[i, rows, :]
            if step == 0 and s == 0:
                y = twice_cdf(jnp.maximum(scale * limit_0[here, :], FLOOR))
                y = jnp.concatenate([y, y], axis=1)
            else:
                scale = jnp.concatenate([scale, scale], axis=1)
                y = twice_cdf(jnp.maximum(scale * acc[h][here, :], FLOOR))
            if step == 0:
                g = gen_b[here, :]
                g = jnp.concatenate([g, g], axis=1)
                n = (
                    lax.broadcasted_iota(jnp.int32, (CHUNK, HALF), 1)
                    + (samp * COLS + h * HALF)
                )
                residue = jnp.bitwise_and(g * n, TOTAL - 1).astype(jnp.float32)
                u = residue * (0.5 * K / TOTAL) + 0.25 * K / TOTAL
                points[i, rows, cols] = u
            else:
                u = points[i, rows, cols]
            coefs = [table[j] for j in range(9)]
            draw[h][par, rows, :] = quantile(u * y, coefs).astype(jnp.bfloat16)
            if step == 2:
                group.append(y[:8] * y[8:])
                if len(group) == 2:
                    term = jnp.log2(group[0] * group[1])
                    total = term if total is None else total + term
                    group = []
        if step == 2:
            if s == 0:
                log_sum[h][i] = total
            else:
                log_sum[h][i] += total

    units = [(s, h) for s in range(M // SUB) for h in range(2)]

    def leaf_pass(step, i, hooks, limit_0=None):
        gen_b = None
        for at, (s, h) in enumerate(units):
            if at in hooks:
                hooks[at]()
            if at + 1 < len(units):
                if step > 0 or units[at + 1][0] > 0:
                    product(step, i, *units[at + 1])
            elif step > 0:
                product(step, jnp.minimum(i + 1, LEAVES - 1), *units[0])
            if step == 0 and h == 0:
                row = gens[i, :, s * SUB : (s + 1) * SUB].astype(jnp.float32)
                gen_b = spread(row).astype(jnp.int32)
            elementwise(step, i, s, h, gen_b, limit_0)

    def contract(basis, i, par):
        both = jnp.concatenate([draw_0[par], draw_1[par]], axis=1)
        return jnp.dot(basis[i], both, preferred_element_type=jnp.float32)

    def first_coef(i, par):
        first_send[i] = contract(row_one, i, par).astype(jnp.bfloat16)

    def second_coef(i, par):
        second_send[i] = contract(row_two, i, par)

    last = LEAVES - 1

    def pass_a(i, carry):
        for which in (0, 1, 3, 4):
            load(which, i).wait()
        before = jnp.maximum(i - 1, 0)
        first_coef(before, lax.rem(i + 1, 2))
        limit = -limits[i]
        high = limit.astype(jnp.bfloat16)
        rest = limit - high.astype(jnp.float32)
        mid = rest.astype(jnp.bfloat16)
        tiny = (rest - mid.astype(jnp.float32)).astype(jnp.bfloat16)
        at = lax.broadcasted_iota(jnp.int32, (SUB, SUB), 0)
        limit_0 = spread(limit[:, :SUB])
        for s in range(M // SUB):
            rows = slice(s * SUB, (s + 1) * SUB)
            scale_b[i, rows, :] = spread(scales[i, :, rows] * -ROOT_HALF)
            parts = [
                jnp.broadcast_to(v[:, rows].astype(jnp.float32), (SUB, SUB))
                for v in (high, mid, tiny)
            ]
            part = jnp.where(at == 0, parts[0], jnp.where(at == 1, parts[1], parts[2]))
            part = jnp.where(at < 3, part, 0.0).astype(jnp.bfloat16)
            tops[i, rows, :] = part.T
            pair = cols_t[i, :, rows]
            cols_c[i, rows, :] = pair.T
            cols_b[i, rows, :] = jnp.concatenate([pair[:R], part[:R]], axis=0).T

        def send():
            @pl.when(i == 1)
            def _():
                pl.semaphore_wait(barrier, n_leaf + n_samp - 2)

            @pl.when(i >= 1)
            def _():
                first_copy(i - 1).start()

        leaf_pass(0, i, {2: send}, limit_0)
        return carry

    lax.fori_loop(0, LEAVES, pass_a, 0)
    first_coef(last, last % 2)
    first_copy(0).wait_recv()
    product(1, 0, *units[0])

    def pass_b(i, carry):
        load(2, i).wait()

        @pl.when(i < last)
        def _():
            first_copy(i + 1).wait_recv()

        second_coef(jnp.maximum(i - 1, 0), lax.rem(i + 1, 2))

        def send():
            @pl.when(i == 0)
            def _():
                first_copy(last).start()

            @pl.when(i >= 1)
            def _():
                second_copy(i - 1).start()

        def pair():
            @pl.when(i >= 2)
            def _():
                add_pair(i - 2)

        def send_pair():
            @pl.when(i >= 2)
            def _():
                pair_copy(i - 2).start()

        leaf_pass(1, i, {1: pair, 2: send, 3: send_pair})
        return carry

    def add_pair(i):
        second_copy(i).wait_recv()
        pair_send[i] = (second_send[i] + second_recv[i]).astype(jnp.bfloat16)

    lax.fori_loop(0, LEAVES, pass_b, 0)
    second_coef(last, last % 2)
    pair_copy(0).wait_recv()
    product(2, 0, *units[0])

    def pass_c(i, carry):
        @pl.when(i < last)
        def _():
            pair_copy(i + 1).wait_recv()

        @pl.when(i >= 2)
        def _():
            out_copy(i - 2, 0).wait()
            out_copy(i - 2, 1).wait()

        def send():
            @pl.when(i == 0)
            def _():
                second_copy(last).start()

        def pair():
            @pl.when(i < 2)
            def _():
                add_pair(i + LEAVES - 2)

        def send_pair():
            @pl.when(i < 2)
            def _():
                pair_copy(i + LEAVES - 2).start()

        leaf_pass(2, i, {1: pair, 2: send, 3: send_pair})
        out_copy(i, 0).start()
        out_copy(i, 1).start()
        return carry

    lax.fori_loop(0, LEAVES, pass_c, 0)

    logsum = jnp.concatenate(
        [jnp.sum(log_0[...], axis=1), jnp.sum(log_1[...], axis=1)], axis=1
    )
    logsum = (logsum - float(M)) * math.log(2.0)
    peak = jnp.max(logsum, axis=1, keepdims=True)
    mass = jnp.sum(jnp.exp(logsum - peak), axis=1, keepdims=True)
    lane = lax.broadcasted_iota(jnp.int32, (LEAVES, SUB), 1)
    stat_all[samp] = jnp.where(lane == 0, peak, mass)
    sums_all[leaf] = jnp.sum(logsum, axis=0, keepdims=True)

    def stat_copy(d):
        to = lax.rem(samp + d, n_samp)
        return pltpu.make_async_remote_copy(
            src_ref=stat_all.at[samp],
            dst_ref=stat_all.at[samp],
            send_sem=stat_sems.at[0, d],
            recv_sem=stat_sems.at[1, d],
            device_id={"samp": to},
            device_id_type=MESH,
        )

    def sums_copy(d):
        to = lax.rem(leaf + d, n_leaf)
        return pltpu.make_async_remote_copy(
            src_ref=sums_all.at[leaf],
            dst_ref=sums_all.at[leaf],
            send_sem=sums_sems.at[0, d],
            recv_sem=sums_sems.at[1, d],
            device_id={"leaf": to},
            device_id_type=MESH,
        )

    def each(copy, what, count):
        def body(d, carry):
            what(copy(d))
            return carry

        lax.fori_loop(1, count, body, 0)

    each(stat_copy, lambda c: c.start(), n_samp)
    each(sums_copy, lambda c: c.start(), n_leaf)

    def drain(i, carry):
        first_copy(i).wait_send()
        second_copy(i).wait_send()
        pair_copy(i).wait_send()
        return carry

    lax.fori_loop(0, LEAVES, drain, 0)
    for i in (LEAVES - 2, LEAVES - 1):
        out_copy(i, 0).wait()
        out_copy(i, 1).wait()
    each(stat_copy, lambda c: c.wait(), n_samp)
    each(sums_copy, lambda c: c.wait(), n_leaf)

    stats = stat_all[...]
    peaks = stats[:, :, 0:1]
    top = jnp.max(peaks, axis=0)
    whole = jnp.sum(stats[:, :, 1:2] * jnp.exp(peaks - top[None]), axis=0)
    mean = (top + jnp.log(whole / TOTAL)) / M
    mean_out[...] = jnp.broadcast_to(mean, (LEAVES, SUB)).T[0:1]
    total = jnp.sum(sums_all[...], axis=0) / (LEAVES * n_leaf * M)
    sample_out[...] = total.reshape(COLS)


def per_device(limits, inv_scale, lower_blocks, qmc_gen, col_one, row_one, col_two, row_two):
    vmem = pl.BlockSpec(memory_space=pltpu.VMEM)
    anywhere = pl.BlockSpec(memory_space=pl.ANY)
    f32, bf16 = jnp.float32, jnp.bfloat16
    n_leaf, n_samp = lax.axis_size("leaf"), lax.axis_size("samp")
    dma = pltpu.SemaphoreType.DMA
    bases = [jnp.swapaxes(v, 2, 3) for v in (col_one, row_one, col_two, row_two)]
    draws, mean_log, sample_log = pl.pallas_call(
        kernel,
        out_shape=(
            jax.ShapeDtypeStruct((LEAVES, 1, M, COLS), bf16),
            jax.ShapeDtypeStruct((1, LEAVES), f32),
            jax.ShapeDtypeStruct((COLS,), f32),
        ),
        in_specs=[vmem, vmem, anywhere, vmem, anywhere, anywhere, anywhere, anywhere],
        out_specs=(anywhere, vmem, vmem),
        scratch_shapes=[
            pltpu.VMEM((LEAVES, M, M), bf16),
            pltpu.VMEM((LEAVES, 2 * R, M), bf16),
            pltpu.VMEM((LEAVES, R, M), bf16),
            pltpu.VMEM((LEAVES, R, M), bf16),
            pltpu.VMEM((LEAVES, M, 2 * R), bf16),
            pltpu.VMEM((LEAVES, M, 2 * R), bf16),
            pltpu.VMEM((LEAVES, M, SUB), bf16),
            pltpu.VMEM((9, 8, 128), f32),
            pltpu.VMEM((LEAVES, M, COLS), f32),
            pltpu.VMEM((LEAVES, M, SUB), f32),
            pltpu.VMEM((SUB, HALF), f32),
            pltpu.VMEM((SUB, HALF), f32),
            pltpu.VMEM((2, M, HALF), bf16),
            pltpu.VMEM((2, M, HALF), bf16),
            pltpu.VMEM((LEAVES, 8, HALF), f32),
            pltpu.VMEM((LEAVES, 8, HALF), f32),
            pltpu.VMEM((LEAVES, R, COLS), bf16),
            pltpu.VMEM((LEAVES, R, COLS), bf16),
            pltpu.VMEM((LEAVES, R, COLS), f32),
            pltpu.VMEM((LEAVES, R, COLS), f32),
            pltpu.VMEM((LEAVES, R, COLS), bf16),
            pltpu.VMEM((LEAVES, R, COLS), bf16),
            pltpu.VMEM((n_samp, LEAVES, SUB), f32),
            pltpu.VMEM((n_leaf, 1, COLS), f32),
            dma((5, LEAVES)),
            dma((2, LEAVES)),
            dma((2, LEAVES)),
            dma((2, LEAVES)),
            dma((2, LEAVES)),
            dma((2, n_samp)),
            dma((2, n_leaf)),
        ],
        compiler_params=pltpu.CompilerParams(
            collective_id=0, has_side_effects=True, vmem_limit_bytes=60 * 1024 * 1024
        ),
        name="conditioning",
    )(limits, inv_scale, lower_blocks, qmc_gen, *bases)
    return draws, mean_log.T, sample_log


def solution(mesh):
    return jax.shard_map(
        per_device,
        mesh=mesh,
        in_specs=(
            P(None, "leaf", None),
            P(None, "leaf", None),
            P(None, "leaf", None, None),
            P(None, "leaf", None),
            P(None, "leaf", None, None),
            P(None, "leaf", None, None),
            P(None, "leaf", None, None),
            P(None, "leaf", None, None),
        ),
        out_specs=(P(None, "leaf", None, "samp"), P(None, "leaf"), P("samp")),
        check_vma=False,
    )
```

```python
import functools
import math

import jax
import jax.numpy as jnp
from jax import lax
from jax.experimental import pallas as pl
from jax.experimental.pallas import tpu as pltpu
from jax.sharding import PartitionSpec as P

LEAVES = 8
M = 512
R = 64
SUB = 128
COLS = 512
HALF = 256
CHUNK = 16
TOTAL = 8192
MESH = pl.DeviceIdType.MESH

coef_a = (
    -39.69683028665376,
    220.9460984245205,
    -275.9285104469687,
    138.357751867269,
    -30.66479806614716,
    2.506628277459239,
)
coef_b = (
    -54.47609879822406,
    161.5858368580409,
    -155.6989798598866,
    66.80131188771972,
    -13.28068155288572,
    1.0,
)
coef_c = (
    -0.007784894002430293,
    -0.3223964580411365,
    -2.400758277161838,
    -2.549732539343734,
    4.374664141464968,
    2.938163982698783,
)
coef_d = (0.007784695709041462, 0.3224671290700398, 2.445134137142996, 3.754408661907416, 1.0)
split_low = 0.02425

K = coef_a[0] / coef_b[0]
G = math.sqrt(2.0 * math.log(2.0))
EDGE = K * (0.5 - split_low)
TAIL = -coef_c[0] * G / coef_d[0]
mono_a = tuple(v / coef_a[0] * K ** (2 * j) for j, v in enumerate(coef_a))
mono_b = tuple(v / coef_b[0] * K ** (2 * j) for j, v in enumerate(coef_b))
mono_c = tuple(v / coef_c[0] * G**-j for j, v in enumerate(coef_c))
mono_d = tuple(EDGE / TAIL * v / coef_d[0] * G**-j for j, v in enumerate(coef_d))

ROOT_HALF = math.sqrt(0.5)
FLOOR = -6.0 * ROOT_HALF
ERFC_FROM = -3.5 * ROOT_HALF
erfc_log2 = (
    0.001479457231,
    0.02841664334,
    -1.205206352,
    1.255708033,
    -0.2048280003,
)


def twice_cdf(z):
    tail = z * erfc_log2[0] + erfc_log2[1]
    for entry in erfc_log2[2:]:
        tail = tail * z + entry
    return jnp.where(z < ERFC_FROM, lax.exp2(tail), lax.erf(z) + 1.0)


def quantile(p):
    mono = mono_a[1:] + mono_b[2:]
    centre = p - 0.5 * K
    square = centre * centre
    small = jnp.minimum(p, K - p)
    tail = small < K * split_low
    depth = math.log2(K) - jnp.log2(small)
    depth = depth * lax.rsqrt(depth)
    var = jnp.where(tail, depth, square)
    top = var + jnp.where(tail, mono_c[1], mono[0])
    for c, a in zip(mono_c[2:], mono[1:5]):
        top = top * var + jnp.where(tail, c, a)
    low = jnp.where(tail, mono_d[0], square + mono_b[1])
    for d, b in zip(mono_d[1:], mono[5:]):
        low = low * var + jnp.where(tail, d, b)
    scale = jnp.clip(centre, -EDGE, EDGE)
    return scale * top / low


def kernel(
    limits,
    scales,
    lower_hbm,
    gens,
    col_one_hbm,
    row_one_hbm,
    col_two_hbm,
    row_two_hbm,
    draws_hbm,
    mean_out,
    sample_out,
    lower,
    cols_t,
    row_one,
    row_two,
    cols_b,
    cols_c,
    tops,
    points,
    scale_b,
    acc_0,
    acc_1,
    draw_0,
    draw_1,
    log_0,
    log_1,
    first_send,
    first_recv,
    second_send,
    second_recv,
    pair_send,
    pair_recv,
    stat_all,
    sums_all,
    load_sem,
    out_sem,
    first_sems,
    second_sems,
    pair_sems,
    stat_sems,
    sums_sems,
):
    leaf = lax.axis_index("leaf")
    samp = lax.axis_index("samp")
    n_leaf = lax.axis_size("leaf")
    n_samp = lax.axis_size("samp")
    sibling = leaf + 1 - 2 * lax.rem(leaf, 2)
    across = leaf + 2 - 4 * lax.rem(leaf // 2, 2)
    acc = (acc_0, acc_1)
    draw = (draw_0, draw_1)
    log_sum = (log_0, log_1)

    loads = (
        (lower_hbm, lower),
        (row_one_hbm, row_one),
        (row_two_hbm, row_two),
        (col_one_hbm, cols_t),
        (col_two_hbm, cols_t),
    )

    def load(which, i):
        src, dst = loads[which]
        dst = dst.at[i]
        if which == 3:
            dst = dst.at[:R]
        if which == 4:
            dst = dst.at[R:]
        return pltpu.make_async_copy(src.at[i, 0], dst, load_sem.at[which, i])

    def start_loads(i, carry):
        for which in (3, 4, 0, 1, 2):
            load(which, i).start()
        return carry

    lax.fori_loop(0, LEAVES, start_loads, 0)
    for h in range(2):
        draw[h][1] = jnp.zeros((M, HALF), jnp.bfloat16)
    row = lax.broadcasted_iota(jnp.int32, (SUB, HALF), 0)
    ones_row = jnp.where(row < 3, 1.0, 0.0).astype(jnp.bfloat16)

    barrier = pltpu.get_barrier_semaphore()

    def greet_leaf(d, carry):
        pl.semaphore_signal(
            barrier, inc=1, device_id={"leaf": lax.rem(leaf + d, n_leaf)}, device_id_type=MESH
        )
        return carry

    def greet_samp(d, carry):
        pl.semaphore_signal(
            barrier, inc=1, device_id={"samp": lax.rem(samp + d, n_samp)}, device_id_type=MESH
        )
        return carry

    lax.fori_loop(1, n_leaf, greet_leaf, 0)
    lax.fori_loop(1, n_samp, greet_samp, 0)

    def first_copy(i):
        return pltpu.make_async_remote_copy(
            src_ref=first_send.at[i],
            dst_ref=first_recv.at[i],
            send_sem=first_sems.at[0, i],
            recv_sem=first_sems.at[1, i],
            device_id={"leaf": sibling},
            device_id_type=MESH,
        )

    def second_copy(i):
        return pltpu.make_async_remote_copy(
            src_ref=second_send.at[i],
            dst_ref=second_recv.at[i],
            send_sem=second_sems.at[0, i],
            recv_sem=second_sems.at[1, i],
            device_id={"leaf": sibling},
            device_id_type=MESH,
        )

    def pair_copy(i):
        return pltpu.make_async_remote_copy(
            src_ref=pair_send.at[i],
            dst_ref=pair_recv.at[i],
            send_sem=pair_sems.at[0, i],
            recv_sem=pair_sems.at[1, i],
            device_id={"leaf": across},
            device_id_type=MESH,
        )

    def out_copy(i, h):
        return pltpu.make_async_copy(
            draw[h].at[lax.rem(i, 2)],
            draws_hbm.at[i, 0, :, pl.ds(h * HALF, HALF)],
            out_sem.at[h, i],
        )

    def spread(row):
        return jnp.broadcast_to(row, (SUB, SUB)).T

    def product(step, i, s, h):
        rows = slice(s * SUB, (s + 1) * SUB)
        cols = slice(h * HALF, (h + 1) * HALF)
        left, right = [], []
        if step == 1:
            left.append(cols_b[i, rows, :])
            right += [first_recv[i, :, cols], ones_row[:R]]
        if step == 2:
            left.append(cols_c[i, rows, :])
            right += [first_recv[i, :, cols], pair_recv[i, :, cols]]
        if step != 1:
            left.append(tops[i, rows, :])
            right.append(ones_row)
        if s > 0:
            left.append(lower[i, rows, : s * SUB])
            right.append(draw[h][lax.rem(i, 2), : s * SUB, :])
        a = left[0] if len(left) == 1 else jnp.concatenate(left, axis=1)
        b = right[0] if len(right) == 1 else jnp.concatenate(right, axis=0)
        acc[h][...] = jnp.dot(a, b, preferred_element_type=jnp.float32)

    def elementwise(step, i, s, h, gen_b, limit_0):
        par = lax.rem(i, 2)
        total = None
        group = []
        for chunk in range(SUB // CHUNK):
            at = s * SUB + chunk * CHUNK
            rows = slice(at, at + CHUNK)
            cols = slice(h * HALF, (h + 1) * HALF)
            here = slice(chunk * CHUNK, (chunk + 1) * CHUNK)
            scale = scale_b[i, rows, :]
            if step == 0 and s == 0:
                y = twice_cdf(jnp.maximum(scale * limit_0[here, :], FLOOR))
                y = jnp.concatenate([y, y], axis=1)
            else:
                scale = jnp.concatenate([scale, scale], axis=1)
                y = twice_cdf(jnp.maximum(scale * acc[h][here, :], FLOOR))
            if step == 0:
                g = gen_b[here, :]
                g = jnp.concatenate([g, g], axis=1)
                n = (
                    lax.broadcasted_iota(jnp.int32, (CHUNK, HALF), 1)
                    + (samp * COLS + h * HALF)
                )
                residue = jnp.bitwise_and(g * n, TOTAL - 1).astype(jnp.float32)
                u = residue * (0.5 * K / TOTAL) + 0.25 * K / TOTAL
                points[i, rows, cols] = u
            else:
                u = points[i, rows, cols]
            draw[h][par, rows, :] = quantile(u * y).astype(jnp.bfloat16)
            if step == 2:
                group.append(y[:8] * y[8:])
                if len(group) == 2:
                    term = jnp.log2(group[0] * group[1])
                    total = term if total is None else total + term
                    group = []
        if step == 2:
            if s == 0:
                log_sum[h][i] = total
            else:
                log_sum[h][i] += total

    units = [(s, h) for s in range(M // SUB) for h in range(2)]

    def leaf_pass(step, i, limit_0=None):
        gen_b = None
        for at, (s, h) in enumerate(units):
            if at + 1 < len(units):
                if step > 0 or units[at + 1][0] > 0:
                    product(step, i, *units[at + 1])
            elif step > 0:
                product(step, jnp.minimum(i + 1, LEAVES - 1), *units[0])
            if step == 0 and h == 0:
                row = gens[i, :, s * SUB : (s + 1) * SUB].astype(jnp.float32)
                gen_b = spread(row).astype(jnp.int32)
            elementwise(step, i, s, h, gen_b, limit_0)

    def contract(basis, i, par):
        both = jnp.concatenate([draw_0[par], draw_1[par]], axis=1)
        return jnp.dot(basis[i], both, preferred_element_type=jnp.float32)

    def first_coef(i, par):
        first_send[i] = contract(row_one, i, par).astype(jnp.bfloat16)

    def second_coef(i, par):
        second_send[i] = contract(row_two, i, par)

    last = LEAVES - 1

    def pass_a(i, carry):
        for which in (0, 1, 3, 4):
            load(which, i).wait()

        @pl.when(i == 2)
        def _():
            pl.semaphore_wait(barrier, n_leaf + n_samp - 2)

        @pl.when(i >= 2)
        def _():
            first_copy(i - 2).start()

        before = jnp.maximum(i - 1, 0)
        first_coef(before, lax.rem(i + 1, 2))
        limit = -limits[i]
        high = limit.astype(jnp.bfloat16)
        rest = limit - high.astype(jnp.float32)
        mid = rest.astype(jnp.bfloat16)
        tiny = (rest - mid.astype(jnp.float32)).astype(jnp.bfloat16)
        at = lax.broadcasted_iota(jnp.int32, (SUB, SUB), 0)
        limit_0 = spread(limit[:, :SUB])
        for s in range(M // SUB):
            rows = slice(s * SUB, (s + 1) * SUB)
            scale_b[i, rows, :] = spread(scales[i, :, rows] * -ROOT_HALF)
            parts = [
                jnp.broadcast_to(v[:, rows].astype(jnp.float32), (SUB, SUB))
                for v in (high, mid, tiny)
            ]
            part = jnp.where(at == 0, parts[0], jnp.where(at == 1, parts[1], parts[2]))
            part = jnp.where(at < 3, part, 0.0).astype(jnp.bfloat16)
            tops[i, rows, :] = part.T
            pair = cols_t[i, :, rows]
            cols_c[i, rows, :] = pair.T
            cols_b[i, rows, :] = jnp.concatenate([pair[:R], part[:R]], axis=0).T

        leaf_pass(0, i, limit_0)
        return carry

    lax.fori_loop(0, LEAVES, pass_a, 0)
    first_copy(last - 1).start()
    first_coef(last, last % 2)
    first_copy(0).wait_recv()
    product(1, 0, *units[0])

    def pass_b(i, carry):
        load(2, i).wait()

        @pl.when(i < last)
        def _():
            first_copy(i + 1).wait_recv()

        @pl.when(i == 0)
        def _():
            first_copy(last).start()

        @pl.when(i >= 2)
        def _():
            second_copy(i - 2).start()

        @pl.when(i >= 4)
        def _():
            pair_copy(i - 4).start()

        @pl.when(i >= 3)
        def _():
            add_pair(i - 3)

        second_coef(jnp.maximum(i - 1, 0), lax.rem(i + 1, 2))
        leaf_pass(1, i)
        return carry

    def add_pair(i):
        second_copy(i).wait_recv()
        pair_send[i] = (second_send[i] + second_recv[i]).astype(jnp.bfloat16)

    lax.fori_loop(0, LEAVES, pass_b, 0)
    second_coef(last, last % 2)
    pair_copy(0).wait_recv()
    product(2, 0, *units[0])

    def pass_c(i, carry):
        @pl.when(i < last)
        def _():
            pair_copy(i + 1).wait_recv()

        @pl.when(i >= 2)
        def _():
            out_copy(i - 2, 0).wait()
            out_copy(i - 2, 1).wait()

        @pl.when(i < 2)
        def _():
            second_copy(i + LEAVES - 2).start()

        @pl.when(i < 4)
        def _():
            pair_copy(i + LEAVES - 4).start()

        @pl.when(i < 3)
        def _():
            add_pair(i + LEAVES - 3)

        leaf_pass(2, i)
        out_copy(i, 0).start()
        out_copy(i, 1).start()
        return carry

    lax.fori_loop(0, LEAVES, pass_c, 0)

    logsum = jnp.concatenate(
        [jnp.sum(log_0[...], axis=1), jnp.sum(log_1[...], axis=1)], axis=1
    )
    logsum = (logsum - float(M)) * math.log(2.0)
    peak = jnp.max(logsum, axis=1, keepdims=True)
    mass = jnp.sum(jnp.exp(logsum - peak), axis=1, keepdims=True)
    lane = lax.broadcasted_iota(jnp.int32, (LEAVES, SUB), 1)
    stat_all[samp] = jnp.where(lane == 0, peak, mass)
    sums_all[leaf] = jnp.sum(logsum, axis=0, keepdims=True)

    def stat_copy(d):
        to = lax.rem(samp + d, n_samp)
        return pltpu.make_async_remote_copy(
            src_ref=stat_all.at[samp],
            dst_ref=stat_all.at[samp],
            send_sem=stat_sems.at[0, d],
            recv_sem=stat_sems.at[1, d],
            device_id={"samp": to},
            device_id_type=MESH,
        )

    def sums_copy(d):
        to = lax.rem(leaf + d, n_leaf)
        return pltpu.make_async_remote_copy(
            src_ref=sums_all.at[leaf],
            dst_ref=sums_all.at[leaf],
            send_sem=sums_sems.at[0, d],
            recv_sem=sums_sems.at[1, d],
            device_id={"leaf": to},
            device_id_type=MESH,
        )

    def each(copy, what, count):
        def body(d, carry):
            what(copy(d))
            return carry

        lax.fori_loop(1, count, body, 0)

    each(stat_copy, lambda c: c.start(), n_samp)
    each(sums_copy, lambda c: c.start(), n_leaf)

    def drain(i, carry):
        first_copy(i).wait_send()
        second_copy(i).wait_send()
        pair_copy(i).wait_send()
        return carry

    lax.fori_loop(0, LEAVES, drain, 0)
    for i in (LEAVES - 2, LEAVES - 1):
        out_copy(i, 0).wait()
        out_copy(i, 1).wait()
    each(stat_copy, lambda c: c.wait(), n_samp)
    each(sums_copy, lambda c: c.wait(), n_leaf)

    stats = stat_all[...]
    peaks = stats[:, :, 0:1]
    top = jnp.max(peaks, axis=0)
    whole = jnp.sum(stats[:, :, 1:2] * jnp.exp(peaks - top[None]), axis=0)
    mean = (top + jnp.log(whole / TOTAL)) / M
    mean_out[...] = jnp.broadcast_to(mean, (LEAVES, SUB)).T[0:1]
    total = jnp.sum(sums_all[...], axis=0) / (LEAVES * n_leaf * M)
    sample_out[...] = total.reshape(COLS)


def per_device(limits, inv_scale, lower_blocks, qmc_gen, col_one, row_one, col_two, row_two):
    vmem = pl.BlockSpec(memory_space=pltpu.VMEM)
    anywhere = pl.BlockSpec(memory_space=pl.ANY)
    f32, bf16 = jnp.float32, jnp.bfloat16
    n_leaf, n_samp = lax.axis_size("leaf"), lax.axis_size("samp")
    dma = pltpu.SemaphoreType.DMA
    bases = [jnp.swapaxes(v, 2, 3) for v in (col_one, row_one, col_two, row_two)]
    draws, mean_log, sample_log = pl.pallas_call(
        kernel,
        out_shape=(
            jax.ShapeDtypeStruct((LEAVES, 1, M, COLS), bf16),
            jax.ShapeDtypeStruct((1, LEAVES), f32),
            jax.ShapeDtypeStruct((COLS,), f32),
        ),
        in_specs=[vmem, vmem, anywhere, vmem, anywhere, anywhere, anywhere, anywhere],
        out_specs=(anywhere, vmem, vmem),
        scratch_shapes=[
            pltpu.VMEM((LEAVES, M, M), bf16),
            pltpu.VMEM((LEAVES, 2 * R, M), bf16),
            pltpu.VMEM((LEAVES, R, M), bf16),
            pltpu.VMEM((LEAVES, R, M), bf16),
            pltpu.VMEM((LEAVES, M, 2 * R), bf16),
            pltpu.VMEM((LEAVES, M, 2 * R), bf16),
            pltpu.VMEM((LEAVES, M, SUB), bf16),
            pltpu.VMEM((LEAVES, M, COLS), f32),
            pltpu.VMEM((LEAVES, M, SUB), f32),
            pltpu.VMEM((SUB, HALF), f32),
            pltpu.VMEM((SUB, HALF), f32),
            pltpu.VMEM((2, M, HALF), bf16),
            pltpu.VMEM((2, M, HALF), bf16),
            pltpu.VMEM((LEAVES, 8, HALF), f32),
            pltpu.VMEM((LEAVES, 8, HALF), f32),
            pltpu.VMEM((LEAVES, R, COLS), bf16),
            pltpu.VMEM((LEAVES, R, COLS), bf16),
            pltpu.VMEM((LEAVES, R, COLS), f32),
            pltpu.VMEM((LEAVES, R, COLS), f32),
            pltpu.VMEM((LEAVES, R, COLS), bf16),
            pltpu.VMEM((LEAVES, R, COLS), bf16),
            pltpu.VMEM((n_samp, LEAVES, SUB), f32),
            pltpu.VMEM((n_leaf, 1, COLS), f32),
            dma((5, LEAVES)),
            dma((2, LEAVES)),
            dma((2, LEAVES)),
            dma((2, LEAVES)),
            dma((2, LEAVES)),
            dma((2, n_samp)),
            dma((2, n_leaf)),
        ],
        compiler_params=pltpu.CompilerParams(
            collective_id=0, has_side_effects=True, vmem_limit_bytes=60 * 1024 * 1024
        ),
        name="conditioning",
    )(limits, inv_scale, lower_blocks, qmc_gen, *bases)
    return draws, mean_log.T, sample_log


def solution(mesh):
    return jax.shard_map(
        per_device,
        mesh=mesh,
        in_specs=(
            P(None, "leaf", None),
            P(None, "leaf", None),
            P(None, "leaf", None, None),
            P(None, "leaf", None),
            P(None, "leaf", None, None),
            P(None, "leaf", None, None),
            P(None, "leaf", None, None),
            P(None, "leaf", None, None),
        ),
        out_specs=(P(None, "leaf", None, "samp"), P(None, "leaf"), P("samp")),
        check_vma=False,
    )
```

```python
import functools
import math

import jax
import jax.numpy as jnp
from jax import lax
from jax.experimental import pallas as pl
from jax.experimental.pallas import tpu as pltpu
from jax.sharding import PartitionSpec as P

LEAVES = 8
M = 512
R = 64
SUB = 128
COLS = 512
HALF = 256
CHUNK = 16
TOTAL = 8192
MESH = pl.DeviceIdType.MESH

coef_a = (
    -39.69683028665376,
    220.9460984245205,
    -275.9285104469687,
    138.357751867269,
    -30.66479806614716,
    2.506628277459239,
)
coef_b = (
    -54.47609879822406,
    161.5858368580409,
    -155.6989798598866,
    66.80131188771972,
    -13.28068155288572,
    1.0,
)
coef_c = (
    -0.007784894002430293,
    -0.3223964580411365,
    -2.400758277161838,
    -2.549732539343734,
    4.374664141464968,
    2.938163982698783,
)
coef_d = (0.007784695709041462, 0.3224671290700398, 2.445134137142996, 3.754408661907416, 1.0)
split_low = 0.02425

K = coef_a[0] / coef_b[0]
G = math.sqrt(2.0 * math.log(2.0))
EDGE = K * (0.5 - split_low)
TAIL = -coef_c[0] * G / coef_d[0]
mono_a = tuple(v / coef_a[0] * K ** (2 * j) for j, v in enumerate(coef_a))
mono_b = tuple(v / coef_b[0] * K ** (2 * j) for j, v in enumerate(coef_b))
mono_c = tuple(v / coef_c[0] * G**-j for j, v in enumerate(coef_c))
mono_d = tuple(EDGE / TAIL * v / coef_d[0] * G**-j for j, v in enumerate(coef_d))


def fewer_products(mono):
    def shifted(by):
        out = list(mono)
        for stop in range(len(out), 1, -1):
            for j in range(1, stop):
                out[j] -= by * out[j - 1]
        return out

    def gap(by):
        q = shifted(by)
        return q[3] - q[1] * q[2]

    low, high = -64.0, 64.0
    rising = gap(high) > gap(low)
    for _ in range(200):
        middle = 0.5 * (low + high)
        if (gap(middle) > 0.0) == rising:
            high = middle
        else:
            low = middle
    q = shifted(low)
    return (low, q[2], q[4], q[1] + low, q[5] - q[4] * q[1])


top_a = fewer_products(mono_a)
top_c = fewer_products(mono_c)

ROOT_HALF = math.sqrt(0.5)
FLOOR = -6.0 * ROOT_HALF
ERFC_FROM = -3.5 * ROOT_HALF
erfc_log2 = (
    0.001479457231,
    0.02841664334,
    -1.205206352,
    1.255708033,
    -0.2048280003,
)


def twice_cdf(z):
    tail = z * erfc_log2[0] + erfc_log2[1]
    for entry in erfc_log2[2:]:
        tail = tail * z + entry
    return jnp.where(z < ERFC_FROM, lax.exp2(tail), lax.erf(z) + 1.0)


def quantile(p, held):
    centre = p - 0.5 * K
    square = centre * centre
    small = jnp.minimum(p, K - p)
    tail = small < K * split_low
    depth = math.log2(K) - jnp.log2(small)
    depth = depth * lax.rsqrt(depth)
    var = jnp.where(tail, depth, square)
    e = [jnp.where(tail, c, a) for c, a in zip(top_c, (held[0], held[1], held[2], held[3], held[4]))]
    y = var + e[0]
    y = y * y
    top = ((y + e[1]) * y + e[2]) * (var + e[3]) + e[4]
    low = jnp.where(tail, mono_d[0], square + mono_b[1])
    for d, b in zip(mono_d[1:], (mono_b[2], mono_b[3], mono_b[4], mono_b[5])):
        low = low * var + jnp.where(tail, d, b)
    scale = jnp.clip(centre, -EDGE, EDGE)
    return scale * top / low


def kernel(
    limits_hbm,
    scales_hbm,
    lower_hbm,
    gens_hbm,
    col_one_hbm,
    row_one_hbm,
    col_two_hbm,
    row_two_hbm,
    draws_hbm,
    mean_out,
    sample_out,
    limits,
    scales,
    gens,
    lower,
    cols_t,
    row_one,
    row_two,
    cols_b,
    cols_c,
    tops,
    table,
    points,
    scale_b,
    cdf_0,
    acc_0,
    acc_1,
    draw_0,
    draw_1,
    log_0,
    log_1,
    first_send,
    first_recv,
    second_send,
    second_recv,
    pair_send,
    pair_recv,
    stat_all,
    sums_all,
    row_sem,
    load_sem,
    out_sem,
    first_sems,
    second_sems,
    pair_sems,
    stat_sems,
    sums_sems,
):
    leaf = lax.axis_index("leaf")
    samp = lax.axis_index("samp")
    n_leaf = lax.axis_size("leaf")
    n_samp = lax.axis_size("samp")
    sibling = leaf + 1 - 2 * lax.rem(leaf, 2)
    across = leaf + 2 - 4 * lax.rem(leaf // 2, 2)
    acc = (acc_0, acc_1)
    draw = (draw_0, draw_1)
    log_sum = (log_0, log_1)

    loads = (
        (lower_hbm, lower),
        (row_one_hbm, row_one),
        (row_two_hbm, row_two),
        (col_one_hbm, cols_t),
        (col_two_hbm, cols_t),
    )

    def load(which, i):
        src, dst = loads[which]
        dst = dst.at[i]
        if which == 3:
            dst = dst.at[:R]
        if which == 4:
            dst = dst.at[R:]
        return pltpu.make_async_copy(src.at[i, 0], dst, load_sem.at[which, i])

    def start_loads(i, carry):
        for which in (3, 4, 0, 1, 2):
            load(which, i).start()
        return carry

    row_loads = [
        pltpu.make_async_copy(src, dst, row_sem.at[at])
        for at, (src, dst) in enumerate(
            ((limits_hbm, limits), (scales_hbm, scales), (gens_hbm, gens))
        )
    ]
    for copy in row_loads:
        copy.start()
    lax.fori_loop(0, LEAVES, start_loads, 0)
    for at, value in enumerate((top_a[0], top_a[1], top_a[2], top_a[3], top_a[4],)):
        table[at] = jnp.full((CHUNK, HALF), value, jnp.float32)
    for h in range(2):
        draw[h][1] = jnp.zeros((M, HALF), jnp.bfloat16)
    row = lax.broadcasted_iota(jnp.int32, (SUB, HALF), 0)
    ones_row = jnp.where(row < 3, 1.0, 0.0).astype(jnp.bfloat16)

    barrier = pltpu.get_barrier_semaphore()

    def greet_leaf(d, carry):
        pl.semaphore_signal(
            barrier, inc=1, device_id={"leaf": lax.rem(leaf + d, n_leaf)}, device_id_type=MESH
        )
        return carry

    def greet_samp(d, carry):
        pl.semaphore_signal(
            barrier, inc=1, device_id={"samp": lax.rem(samp + d, n_samp)}, device_id_type=MESH
        )
        return carry

    lax.fori_loop(1, n_leaf, greet_leaf, 0)
    lax.fori_loop(1, n_samp, greet_samp, 0)

    def first_copy(i):
        return pltpu.make_async_remote_copy(
            src_ref=first_send.at[i],
            dst_ref=first_recv.at[i],
            send_sem=first_sems.at[0, i],
            recv_sem=first_sems.at[1, i],
            device_id={"leaf": sibling},
            device_id_type=MESH,
        )

    def second_copy(i):
        return pltpu.make_async_remote_copy(
            src_ref=second_send.at[i],
            dst_ref=second_recv.at[i],
            send_sem=second_sems.at[0, i],
            recv_sem=second_sems.at[1, i],
            device_id={"leaf": sibling},
            device_id_type=MESH,
        )

    def pair_copy(i):
        return pltpu.make_async_remote_copy(
            src_ref=pair_send.at[i],
            dst_ref=pair_recv.at[i],
            send_sem=pair_sems.at[0, i],
            recv_sem=pair_sems.at[1, i],
            device_id={"leaf": across},
            device_id_type=MESH,
        )

    def out_copy(i, h):
        return pltpu.make_async_copy(
            draw[h].at[lax.rem(i, 2)],
            draws_hbm.at[i, 0, :, pl.ds(h * HALF, HALF)],
            out_sem.at[h, i],
        )

    def spread(row):
        return jnp.broadcast_to(row, (SUB, SUB)).T

    def product(step, i, s, h):
        rows = slice(s * SUB, (s + 1) * SUB)
        cols = slice(h * HALF, (h + 1) * HALF)
        left, right = [], []
        if step == 1:
            left.append(cols_b[i, rows, :])
            right += [first_recv[i, :, cols], ones_row[:R]]
        if step == 2:
            left.append(cols_c[i, rows, :])
            right += [first_recv[i, :, cols], pair_recv[i, :, cols]]
        if step != 1:
            left.append(tops[i, rows, :])
            right.append(ones_row)
        if s > 0:
            left.append(lower[i, rows, : s * SUB])
            right.append(draw[h][lax.rem(i, 2), : s * SUB, :])
        a = left[0] if len(left) == 1 else jnp.concatenate(left, axis=1)
        b = right[0] if len(right) == 1 else jnp.concatenate(right, axis=0)
        acc[h][...] = jnp.dot(a, b, preferred_element_type=jnp.float32)

    def elementwise(step, i, s, h, gen_b, limit_0):
        par = lax.rem(i, 2)
        total = None
        group = []
        for chunk in range(SUB // CHUNK):
            at = s * SUB + chunk * CHUNK
            rows = slice(at, at + CHUNK)
            cols = slice(h * HALF, (h + 1) * HALF)
            here = slice(chunk * CHUNK, (chunk + 1) * CHUNK)
            scale = scale_b[i, rows, :]
            if step == 0 and s == 0:
                if h == 0:
                    y = twice_cdf(jnp.maximum(scale * limit_0[here, :], FLOOR))
                    cdf_0[here, :] = y
                else:
                    y = cdf_0[here, :]
                y = jnp.concatenate([y, y], axis=1)
            else:
                scale = jnp.concatenate([scale, scale], axis=1)
                y = twice_cdf(jnp.maximum(scale * acc[h][here, :], FLOOR))
            if step == 0:
                g = gen_b[here, :]
                g = jnp.concatenate([g, g], axis=1)
                n = (
                    lax.broadcasted_iota(jnp.int32, (CHUNK, HALF), 1)
                    + (samp * COLS + h * HALF)
                )
                residue = jnp.bitwise_and(g * n, TOTAL - 1).astype(jnp.float32)
                u = residue * (0.5 * K / TOTAL) + 0.25 * K / TOTAL
                points[i, rows, cols] = u
            else:
                u = points[i, rows, cols]
            draw[h][par, rows, :] = quantile(u * y, [table[j] for j in range(5)]).astype(jnp.bfloat16)
            if step == 2:
                group.append(y[:8] * y[8:])
                if len(group) == 2:
                    term = jnp.log2(group[0] * group[1])
                    total = term if total is None else total + term
                    group = []
        if step == 2:
            if s == 0:
                log_sum[h][i] = total
            else:
                log_sum[h][i] += total

    units = [(s, h) for s in range(M // SUB) for h in range(2)]

    def leaf_pass(step, i, limit_0=None):
        gen_b = None
        for at, (s, h) in enumerate(units):
            if at + 1 < len(units):
                if step > 0 or units[at + 1][0] > 0:
                    product(step, i, *units[at + 1])
            elif step > 0:
                product(step, jnp.minimum(i + 1, LEAVES - 1), *units[0])
            if step == 0 and h == 0:
                row = gens[i, :, s * SUB : (s + 1) * SUB].astype(jnp.float32)
                gen_b = spread(row).astype(jnp.int32)
            elementwise(step, i, s, h, gen_b, limit_0)

    def contract(basis, i, par):
        both = jnp.concatenate([draw_0[par], draw_1[par]], axis=1)
        return jnp.dot(basis[i], both, preferred_element_type=jnp.float32)

    def first_coef(i, par):
        first_send[i] = contract(row_one, i, par).astype(jnp.bfloat16)

    def second_coef(i, par):
        second_send[i] = contract(row_two, i, par)

    last = LEAVES - 1

    def pass_a(i, carry):
        for which in (0, 1, 3, 4):
            load(which, i).wait()

        @pl.when(i == 2)
        def _():
            pl.semaphore_wait(barrier, n_leaf + n_samp - 2)

        @pl.when(i >= 2)
        def _():
            first_copy(i - 2).start()

        before = jnp.maximum(i - 1, 0)
        first_coef(before, lax.rem(i + 1, 2))
        limit = -limits[i]
        high = limit.astype(jnp.bfloat16)
        rest = limit - high.astype(jnp.float32)
        mid = rest.astype(jnp.bfloat16)
        tiny = (rest - mid.astype(jnp.float32)).astype(jnp.bfloat16)
        at = lax.broadcasted_iota(jnp.int32, (SUB, SUB), 0)
        limit_0 = spread(limit[:, :SUB])
        for s in range(M // SUB):
            rows = slice(s * SUB, (s + 1) * SUB)
            scale_b[i, rows, :] = spread(scales[i, :, rows] * -ROOT_HALF)
            parts = [
                jnp.broadcast_to(v[:, rows].astype(jnp.float32), (SUB, SUB))
                for v in (high, mid, tiny)
            ]
            part = jnp.where(at == 0, parts[0], jnp.where(at == 1, parts[1], parts[2]))
            part = jnp.where(at < 3, part, 0.0).astype(jnp.bfloat16)
            tops[i, rows, :] = part.T
            pair = cols_t[i, :, rows]
            cols_c[i, rows, :] = pair.T
            cols_b[i, rows, :] = jnp.concatenate([pair[:R], part[:R]], axis=0).T

        leaf_pass(0, i, limit_0)
        return carry

    for copy in row_loads:
        copy.wait()
    lax.fori_loop(0, LEAVES, pass_a, 0)
    first_copy(last - 1).start()
    first_coef(last, last % 2)
    first_copy(0).wait_recv()
    product(1, 0, *units[0])

    def pass_b(i, carry):
        load(2, i).wait()

        @pl.when(i < last)
        def _():
            first_copy(i + 1).wait_recv()

        @pl.when(i == 0)
        def _():
            first_copy(last).start()

        @pl.when(i >= 2)
        def _():
            second_copy(i - 2).start()

        @pl.when(i >= 4)
        def _():
            pair_copy(i - 4).start()

        @pl.when(i >= 3)
        def _():
            add_pair(i - 3)

        second_coef(jnp.maximum(i - 1, 0), lax.rem(i + 1, 2))
        leaf_pass(1, i)
        return carry

    def add_pair(i):
        second_copy(i).wait_recv()
        pair_send[i] = (second_send[i] + second_recv[i]).astype(jnp.bfloat16)

    lax.fori_loop(0, LEAVES, pass_b, 0)
    second_coef(last, last % 2)
    pair_copy(0).wait_recv()
    product(2, 0, *units[0])

    def pass_c(i, carry):
        @pl.when(i < last)
        def _():
            pair_copy(i + 1).wait_recv()

        @pl.when(i >= 2)
        def _():
            out_copy(i - 2, 0).wait()
            out_copy(i - 2, 1).wait()

        @pl.when(i < 2)
        def _():
            second_copy(i + LEAVES - 2).start()

        @pl.when(i < 4)
        def _():
            pair_copy(i + LEAVES - 4).start()

        @pl.when(i < 3)
        def _():
            add_pair(i + LEAVES - 3)

        leaf_pass(2, i)
        out_copy(i, 0).start()
        out_copy(i, 1).start()
        return carry

    lax.fori_loop(0, LEAVES, pass_c, 0)

    logsum = jnp.concatenate(
        [jnp.sum(log_0[...], axis=1), jnp.sum(log_1[...], axis=1)], axis=1
    )
    logsum = (logsum - float(M)) * math.log(2.0)
    peak = jnp.max(logsum, axis=1, keepdims=True)
    mass = jnp.sum(jnp.exp(logsum - peak), axis=1, keepdims=True)
    lane = lax.broadcasted_iota(jnp.int32, (LEAVES, SUB), 1)
    stat_all[samp] = jnp.where(lane == 0, peak, mass)
    sums_all[leaf] = jnp.sum(logsum, axis=0, keepdims=True)

    def stat_copy(d):
        to = lax.rem(samp + d, n_samp)
        return pltpu.make_async_remote_copy(
            src_ref=stat_all.at[samp],
            dst_ref=stat_all.at[samp],
            send_sem=stat_sems.at[0, d],
            recv_sem=stat_sems.at[1, d],
            device_id={"samp": to},
            device_id_type=MESH,
        )

    def sums_copy(d):
        to = lax.rem(leaf + d, n_leaf)
        return pltpu.make_async_remote_copy(
            src_ref=sums_all.at[leaf],
            dst_ref=sums_all.at[leaf],
            send_sem=sums_sems.at[0, d],
            recv_sem=sums_sems.at[1, d],
            device_id={"leaf": to},
            device_id_type=MESH,
        )

    def each(copy, what, count):
        def body(d, carry):
            what(copy(d))
            return carry

        lax.fori_loop(1, count, body, 0)

    each(stat_copy, lambda c: c.start(), n_samp)
    each(sums_copy, lambda c: c.start(), n_leaf)

    def drain(i, carry):
        first_copy(i).wait_send()
        second_copy(i).wait_send()
        pair_copy(i).wait_send()
        return carry

    lax.fori_loop(0, LEAVES, drain, 0)
    for i in (LEAVES - 2, LEAVES - 1):
        out_copy(i, 0).wait()
        out_copy(i, 1).wait()
    each(stat_copy, lambda c: c.wait(), n_samp)
    each(sums_copy, lambda c: c.wait(), n_leaf)

    stats = stat_all[...]
    peaks = stats[:, :, 0:1]
    top = jnp.max(peaks, axis=0)
    whole = jnp.sum(stats[:, :, 1:2] * jnp.exp(peaks - top[None]), axis=0)
    mean = (top + jnp.log(whole / TOTAL)) / M
    mean_out[...] = jnp.broadcast_to(mean, (LEAVES, SUB)).T[0:1]
    total = jnp.sum(sums_all[...], axis=0) / (LEAVES * n_leaf * M)
    sample_out[...] = total.reshape(COLS)


def per_device(limits, inv_scale, lower_blocks, qmc_gen, col_one, row_one, col_two, row_two):
    vmem = pl.BlockSpec(memory_space=pltpu.VMEM)
    anywhere = pl.BlockSpec(memory_space=pl.ANY)
    f32, bf16 = jnp.float32, jnp.bfloat16
    n_leaf, n_samp = lax.axis_size("leaf"), lax.axis_size("samp")
    dma = pltpu.SemaphoreType.DMA
    stay = functools.partial(pltpu.with_memory_space_constraint, memory_space=pltpu.HBM)
    bases = [jnp.swapaxes(v, 2, 3) for v in (col_one, row_one, col_two, row_two)]
    draws, mean_log, sample_log = pl.pallas_call(
        kernel,
        out_shape=(
            jax.ShapeDtypeStruct((LEAVES, 1, M, COLS), bf16),
            jax.ShapeDtypeStruct((1, LEAVES), f32),
            jax.ShapeDtypeStruct((COLS,), f32),
        ),
        in_specs=[anywhere] * 8,
        out_specs=(anywhere, vmem, vmem),
        scratch_shapes=[
            pltpu.VMEM((LEAVES, 1, M), f32),
            pltpu.VMEM((LEAVES, 1, M), f32),
            pltpu.VMEM((LEAVES, 1, M), jnp.int32),
            pltpu.VMEM((LEAVES, M, M), bf16),
            pltpu.VMEM((LEAVES, 2 * R, M), bf16),
            pltpu.VMEM((LEAVES, R, M), bf16),
            pltpu.VMEM((LEAVES, R, M), bf16),
            pltpu.VMEM((LEAVES, M, 2 * R), bf16),
            pltpu.VMEM((LEAVES, M, 2 * R), bf16),
            pltpu.VMEM((LEAVES, M, SUB), bf16),
            pltpu.VMEM((5, CHUNK, HALF), f32),
            pltpu.VMEM((LEAVES, M, COLS), f32),
            pltpu.VMEM((LEAVES, M, SUB), f32),
            pltpu.VMEM((SUB, SUB), f32),
            pltpu.VMEM((SUB, HALF), f32),
            pltpu.VMEM((SUB, HALF), f32),
            pltpu.VMEM((2, M, HALF), bf16),
            pltpu.VMEM((2, M, HALF), bf16),
            pltpu.VMEM((LEAVES, 8, HALF), f32),
            pltpu.VMEM((LEAVES, 8, HALF), f32),
            pltpu.VMEM((LEAVES, R, COLS), bf16),
            pltpu.VMEM((LEAVES, R, COLS), bf16),
            pltpu.VMEM((LEAVES, R, COLS), f32),
            pltpu.VMEM((LEAVES, R, COLS), f32),
            pltpu.VMEM((LEAVES, R, COLS), bf16),
            pltpu.VMEM((LEAVES, R, COLS), bf16),
            pltpu.VMEM((n_samp, LEAVES, SUB), f32),
            pltpu.VMEM((n_leaf, 1, COLS), f32),
            dma((3,)),
            dma((5, LEAVES)),
            dma((2, LEAVES)),
            dma((2, LEAVES)),
            dma((2, LEAVES)),
            dma((2, LEAVES)),
            dma((2, n_samp)),
            dma((2, n_leaf)),
        ],
        compiler_params=pltpu.CompilerParams(
            collective_id=0, has_side_effects=True, vmem_limit_bytes=40 * 1024 * 1024
        ),
        name="conditioning",
    )(*map(stay, (limits, inv_scale, lower_blocks, qmc_gen, *bases)))
    return draws, mean_log.T, sample_log


def solution(mesh):
    return jax.shard_map(
        per_device,
        mesh=mesh,
        in_specs=(
            P(None, "leaf", None),
            P(None, "leaf", None),
            P(None, "leaf", None, None),
            P(None, "leaf", None),
            P(None, "leaf", None, None),
            P(None, "leaf", None, None),
            P(None, "leaf", None, None),
            P(None, "leaf", None, None),
        ),
        out_specs=(P(None, "leaf", None, "samp"), P(None, "leaf"), P("samp")),
        check_vma=False,
    )
```
